256 devices in a mesh: grp: 16 (over z, y_lo), blk: 16 (over y_hi, x, core).
Axes of the slice: x: 4, y: 4 (y_hi: 2, y_lo: 2; y = y_hi * 2 + y_lo), z: 8, core: 2. Of those that a mesh axis runs over, the one named last changes fastest.
Arguments:
- states: bfloat16 [524288, 768], P(('grp', 'blk')), may hold values from -6 to 6
- query_weight: bfloat16 [768, 768], replicated, may hold values from -0.21875 to 0.21875
- attempts: bfloat16 [16384, 768], P(('grp', 'blk')), may hold values from -6 to 6
- attempt_theorem: int32 [16384], P('grp'), may hold values from 0 to 15
- positive: int32 [524288], P(('grp', 'blk')), may hold values from 0 to 1023
Outputs:
- loss: float32 [524288], P(('grp', 'blk'))
- grad_attempts: float32 [16384, 768], P(('grp', 'blk'))
- grad_weight: float32 [768, 768], replicated
The draws below stay inside these ranges and needn't reach their ends.
All inputs are finite; a program needn't handle non-finite values.
Results may differ from the reference program's by a relative error of at most 0.012.
Values may be sent and summed in bfloat16 or wider, within the bound.
No kernel may reach another device: no remote copies, remote signals or barrier semaphores. Data moves between devices by JAX's collectives and lax.ppermute only.
A program may use at most 64 MiB of HBM per device.

```python
import math
import jax
import jax.numpy as jnp
import numpy as np
from jax import lax

VECTOR_DIMENSION = 768
Q_DEV = 2048
SLICE_THEOREMS = 16
ATT_SLICE = 1024
QUERIES = 524288
CANDIDATE_COUNT = 16384
N_GRP = 16
N_BLK = 16


def plant(result, stream_key, low, largest):
    dims = result.shape
    index_at = [jax.random.randint(jax.random.fold_in(stream_key, axis), (), 0, dims[axis]) for axis in range(len(dims))]
    result = result.at[tuple(index_at)].set(low)
    longest = dims.index(max(dims))
    index_at[longest] = (index_at[longest] + 1) % dims[longest]
    return result.at[tuple(index_at)].set(largest)


def steps_of(key, dims, split, least, largest):
    level = 1.0
    for position, blocks in split:
        steps = jax.random.uniform(jax.random.fold_in(jax.random.fold_in(key, 6), position), (blocks,), jnp.float32, least / len(split), largest / len(split))
        level = level * jnp.repeat(jnp.exp(steps), dims[position] // blocks).reshape((-1,) + (1,) * (len(dims) - 1 - position))
    return level


def rank_table(amount, skew):
    portions = [(1 << 20) // math.isqrt(standing ** skew) + 1 for standing in range(1, amount + 1)]
    width = 1 + sum(portions) // (1 << 30)
    return np.cumsum(np.array([max(1, weight // width) for weight in portions]))


def ranked(own_key, extent, amount, slope):
    table = rank_table(amount, slope)
    lot = jax.random.randint(jax.random.fold_in(own_key, 1), extent, 0, int(table[amount - 1]))
    grade = jnp.searchsorted(jnp.asarray(table, jnp.int32), lot, side="right")
    return jax.random.permutation(jax.random.fold_in(own_key, 2), amount)[grade].astype(jnp.int32)


def normal_values(own_key, dims, width, limit, shards=(), dtype=jnp.bfloat16):
    drawn = jax.random.normal(own_key, dims, jnp.float32) * width
    if len(shards) > 0:
        drawn = steps_of(own_key, dims, shards, -0.22, 0.18) * drawn
    return jnp.clip(drawn, min=-limit, max=limit).astype(dtype)


def setup_inputs(seed: int = 0) -> dict:
    streams_of = jax.random.split(jax.random.key(seed), 6)
    states = normal_values(streams_of[0], (QUERIES, VECTOR_DIMENSION), 1.0, 6.0, ((0, 256),))
    query_weight = normal_values(streams_of[1], (VECTOR_DIMENSION, VECTOR_DIMENSION), VECTOR_DIMENSION ** -0.5, 0.21875)
    attempts = normal_values(streams_of[2], (CANDIDATE_COUNT, VECTOR_DIMENSION), 1.0, 6.0, ((0, 256),))
    attempt_theorem = plant(ranked(streams_of[3], (CANDIDATE_COUNT,), SLICE_THEOREMS, 2), jax.random.fold_in(streams_of[3], 3), 0, SLICE_THEOREMS - 1).astype(jnp.int32)
    positive = plant(jax.random.randint(streams_of[4], (QUERIES,), 0, ATT_SLICE), jax.random.fold_in(streams_of[4], 1), 0, ATT_SLICE - 1).astype(jnp.int32)
    return {"states": states, "query_weight": query_weight, "attempts": attempts, "attempt_theorem": attempt_theorem, "positive": positive}


logit_sharpness = 0.07
epsilon = 1e-06

def normalized_rows(values):
    return values * lax.rsqrt(lax.optimization_barrier(jnp.mean(values * values, axis=-1, keepdims=True)) + epsilon)

def reference(states, query_weight, attempts, attempt_theorem, positive):
    logit_multiplier = 1.0 / (logit_sharpness * VECTOR_DIMENSION)
    state_blocks = states.reshape(N_GRP, N_BLK, Q_DEV, VECTOR_DIMENSION)
    attempt_blocks = attempts.reshape(N_GRP, ATT_SLICE, VECTOR_DIMENSION)
    theorem_blocks = attempt_theorem.reshape(N_GRP, ATT_SLICE)
    positive_blocks = positive.reshape(N_GRP, N_BLK, Q_DEV)

    def slice_step(weight_sum, slice_data):
        slice_states, slice_attempts, slice_theorem, slice_positive = slice_data
        attempt_rows_float, attempt_back = jax.vjp(normalized_rows, slice_attempts.astype(jnp.float32))
        candidate_direction = attempt_rows_float.astype(jnp.bfloat16)

        def device_step(grad_sum, device_data):
            dev_states, local_matching_target = device_data
            proj = jnp.dot(dev_states, query_weight, preferred_element_type=jnp.float32)
            query_float, query_back = jax.vjp(normalized_rows, proj)
            query_unit = query_float.astype(jnp.bfloat16)
            anchor_lemma_label = jnp.take(slice_theorem, local_matching_target)
            scores = jnp.dot(query_unit, candidate_direction.T, preferred_element_type=jnp.float32) * logit_multiplier
            mask = anchor_lemma_label[:, None] == slice_theorem[None, :]
            expo = jnp.where(mask, jnp.exp(scores), 0.0)
            total = lax.optimization_barrier(jnp.sum(expo, axis=1))
            columns = lax.broadcasted_iota(jnp.int32, scores.shape, 1)
            chosen = columns == local_matching_target[:, None]
            pos_score = lax.optimization_barrier(jnp.sum(jnp.where(chosen, scores, 0.0), axis=1))
            losses = jnp.log(total) - pos_score
            weights = (expo / total[:, None] - chosen.astype(jnp.float32)).astype(jnp.bfloat16)
            grad_qunit = jnp.dot(weights, candidate_direction, preferred_element_type=jnp.float32) * logit_multiplier
            partial_term = jnp.dot(weights.T, query_unit, preferred_element_type=jnp.float32) * logit_multiplier
            partial_term = lax.optimization_barrier(partial_term.astype(jnp.bfloat16)).astype(jnp.float32)
            grad_proj = query_back(grad_qunit)[0].astype(jnp.bfloat16)
            weight_term = jnp.dot(dev_states.T, grad_proj, preferred_element_type=jnp.float32)
            return (grad_sum + partial_term, (losses, weight_term))
        start = jnp.zeros((ATT_SLICE, VECTOR_DIMENSION), jnp.float32)
        grad_sum, (losses, weight_terms) = lax.scan(device_step, start, (slice_states, slice_positive))
        grad_attempts = attempt_back(grad_sum)[0]
        return (weight_sum + lax.optimization_barrier(jnp.sum(weight_terms, axis=0)), (losses, grad_attempts))
    weight_sum, (losses, grads) = lax.scan(slice_step, jnp.zeros((VECTOR_DIMENSION, VECTOR_DIMENSION), jnp.float32), (state_blocks, attempt_blocks, theorem_blocks, positive_blocks))
    return (losses.reshape(QUERIES), grads.reshape(CANDIDATE_COUNT, VECTOR_DIMENSION), weight_sum)
```

```python
import functools
import itertools

import jax
import jax.numpy as jnp
from jax import lax
from jax.experimental import pallas as pl
from jax.experimental.pallas import tpu as pltpu
from jax.sharding import Mesh, PartitionSpec as P

SHARP = 0.07
EPS = 1e-06
AXES = ("z", "yl", "yh", "x", "c")
SIZES = (8, 2, 2, 4, 2)
PLANE = ("yh", "yl", "x")
CHIPS = [(dy, dx) for dy in range(2) for dx in range(4)]
BF, F32 = jnp.bfloat16, jnp.float32
Q_TILE = 512


def flat(coords):
    index = 0
    for value, size in zip(coords, SIZES):
        index = index * size + value % size
    return index


def send(value, move):
    pairs = [(flat(at), flat(move(*at))) for at in itertools.product(*map(range, SIZES))]
    return lax.ppermute(value, AXES, pairs)


def to_core(value):
    return send(value, lambda z, yl, yh, x, c: (z, yl, yh, x, c ^ 1))


def to_chip(value, dy, dx):
    return send(value, lambda z, yl, yh, x, c: (z, yl, yh ^ dy, x + dx, c))


def to_z(value, bit):
    return send(value, lambda z, yl, yh, x, c: (z ^ bit, yl, yh, x, c))


def proj_kernel(states, weight, proj, query, scale, weight_t):
    @pl.when(pl.program_id(0) == 0)
    def _():
        weight_t[...] = weight[...].T

    p = lax.dot_general(
        weight_t[...], states[...], (((1,), (1,)), ((), ())), preferred_element_type=F32
    )
    r = lax.rsqrt(jnp.sum(p * p, axis=0, keepdims=True) * (1.0 / p.shape[0]) + EPS)
    proj[...] = p
    query[...] = (p * r).astype(BF)
    scale[...] = r


def project(states, weight):
    queries, width = states.shape
    return pl.pallas_call(
        proj_kernel,
        grid=(queries // Q_TILE,),
        in_specs=[
            pl.BlockSpec((Q_TILE, width), lambda i: (i, 0)),
            pl.BlockSpec((width, width), lambda i: (0, 0)),
        ],
        out_specs=[
            pl.BlockSpec((width, Q_TILE), lambda i: (0, i)),
            pl.BlockSpec((width, Q_TILE), lambda i: (0, i)),
            pl.BlockSpec((1, Q_TILE), lambda i: (0, i)),
        ],
        out_shape=[
            jax.ShapeDtypeStruct((width, queries), F32),
            jax.ShapeDtypeStruct((width, queries), BF),
            jax.ShapeDtypeStruct((1, queries), F32),
        ],
        scratch_shapes=[pltpu.VMEM((width, width), BF)],
        cost_estimate=pl.CostEstimate(
            flops=2 * queries * width * width,
            bytes_accessed=queries * width * 8,
            transcendentals=0,
        ),
        name="project",
    )(states, weight)


def loss_kernel(mult, proj, query, scale, own, other, ids, labels, positive,
                loss, weights, grad_proj, own_t, other_t):
    @pl.when(pl.program_id(0) == 0)
    def _():
        own_t[...] = own[...].T
        other_t[...] = other[...].T

    half = own.shape[0]
    q = query[...]
    pos = positive[...]
    label_a, label_b = labels[:half, :], labels[half:, :]
    chosen_a = ids[:half, :] == pos
    chosen_b = ids[half:, :] == pos
    label_q = jnp.sum(jnp.where(chosen_a, label_a, 0.0), axis=0, keepdims=True)
    label_q += jnp.sum(jnp.where(chosen_b, label_b, 0.0), axis=0, keepdims=True)
    s_a = jnp.dot(own[...], q, preferred_element_type=F32) * mult
    s_b = jnp.dot(other[...], q, preferred_element_type=F32) * mult
    pick = jnp.sum(jnp.where(chosen_a, s_a, 0.0), axis=0, keepdims=True)
    pick += jnp.sum(jnp.where(chosen_b, s_b, 0.0), axis=0, keepdims=True)
    e_a = jnp.where(label_a == label_q, jnp.exp(s_a), 0.0)
    e_b = jnp.where(label_b == label_q, jnp.exp(s_b), 0.0)
    total = jnp.sum(e_a, axis=0, keepdims=True) + jnp.sum(e_b, axis=0, keepdims=True)
    loss[...] = jnp.log(total) - pick
    inv = 1.0 / total
    w_a = (e_a * inv - jnp.where(chosen_a, 1.0, 0.0)).astype(BF)
    w_b = (e_b * inv - jnp.where(chosen_b, 1.0, 0.0)).astype(BF)
    weights[:half, :] = w_a
    weights[half:, :] = w_b
    g = jnp.dot(own_t[...], w_a, preferred_element_type=F32)
    g += jnp.dot(other_t[...], w_b, preferred_element_type=F32)
    g = g * mult
    r = scale[...]
    u = proj[...] * r
    inner = jnp.sum(u * g, axis=0, keepdims=True) * (1.0 / u.shape[0])
    grad_proj[...] = ((g - u * inner) * r).astype(BF)


def losses_and_weights(mult, proj, query, scale, own, other, ids, labels, positive):
    width, queries = proj.shape
    half = own.shape[0]
    column = lambda rows: pl.BlockSpec((rows, Q_TILE), lambda i: (0, i))
    whole = lambda shape: pl.BlockSpec(shape, lambda i: (0, 0))
    return pl.pallas_call(
        functools.partial(loss_kernel, mult),
        grid=(queries // Q_TILE,),
        in_specs=[
            column(width), column(width), column(1),
            whole((half, width)), whole((half, width)),
            whole((2 * half, 1)), whole((2 * half, 1)), column(1),
        ],
        out_specs=[column(1), column(2 * half), column(width)],
        out_shape=[
            jax.ShapeDtypeStruct((1, queries), F32),
            jax.ShapeDtypeStruct((2 * half, queries), BF),
            jax.ShapeDtypeStruct((width, queries), BF),
        ],
        scratch_shapes=[pltpu.VMEM((width, half), BF), pltpu.VMEM((width, half), BF)],
        cost_estimate=pl.CostEstimate(
            flops=8 * queries * width * half,
            bytes_accessed=queries * width * 12,
            transcendentals=2 * half * queries,
        ),
        name="losses",
    )(proj, query, scale, own, other, ids, labels, positive)


def on_device(states, query_weight, attempts, attempt_theorem, positive):
    width = states.shape[1]
    mult = 1.0 / (SHARP * width)
    rows = attempts.shape[0]
    yh, x, c = lax.axis_index("yh"), lax.axis_index("x"), lax.axis_index("c")

    a32 = attempts.astype(F32)
    a_scale = lax.rsqrt(jnp.mean(a32 * a32, axis=-1, keepdims=True) + EPS)
    a_unit = a32 * a_scale
    mine = a_unit.astype(BF)
    blocks = [mine] + [to_chip(mine, dy, dx) for dy, dx in CHIPS[1:]]
    own = jnp.concatenate(blocks, axis=0)
    other = to_core(own)

    chip_ids = jnp.stack([(yh ^ dy) * 4 + (x - dx) % 4 for dy, dx in CHIPS])
    block_ids = jnp.concatenate([chip_ids * 2 + c, chip_ids * 2 + (1 - c)])
    ids = (block_ids[:, None] * rows + jnp.arange(rows, dtype=jnp.int32)[None, :]).reshape(-1, 1)
    labels = jnp.take(attempt_theorem.reshape(-1, rows), block_ids, axis=0)
    labels = labels.astype(F32).reshape(-1, 1)

    proj, query, scale = project(states, query_weight)
    loss, weights, grad_proj = losses_and_weights(
        mult, proj, query, scale, own, other, ids, labels, positive.reshape(1, -1)
    )

    grad_w = lax.dot_general(
        states, grad_proj, (((0,), (1,)), ((), ())), preferred_element_type=F32
    )
    half_w = width // 2
    w_keep = lax.dynamic_slice_in_dim(grad_w, c * half_w, half_w, 0)
    w_give = lax.dynamic_slice_in_dim(grad_w, (1 - c) * half_w, half_w, 0).astype(BF)
    w_sum = (w_keep + to_core(w_give).astype(F32)).astype(BF)
    parts = lax.all_to_all(w_sum.reshape(16, -1, width), PLANE, 0, 0)
    piece = jnp.sum(parts.astype(F32), axis=0)
    for bit in (1, 2, 4):
        rounded = piece.astype(BF)
        piece = rounded.astype(F32) + to_z(rounded, bit).astype(F32)
    spread = jnp.broadcast_to(piece.astype(BF)[None], (16,) + piece.shape)
    w_half = lax.all_to_all(spread, PLANE, 0, 0).reshape(half_w, width)
    w_rest = to_core(w_half)
    low = jnp.where(c == 0, w_half, w_rest)
    high = jnp.where(c == 0, w_rest, w_half)
    grad_weight = jnp.concatenate([low, high], axis=0).astype(F32)

    half_a = own.shape[0]
    contract = (((1,), (1,)), ((), ()))
    a_give = lax.dot_general(
        weights[half_a:], query, contract, preferred_element_type=F32
    ).astype(BF)
    a_keep = lax.dot_general(weights[:half_a], query, contract, preferred_element_type=F32)
    a_sum = a_keep + to_core(a_give).astype(F32)
    total = a_sum[:rows]
    for k, (dy, dx) in enumerate(CHIPS[1:], 1):
        total += to_chip(a_sum[k * rows : (k + 1) * rows].astype(BF), dy, -dx).astype(F32)
    g = total * mult
    inner = jnp.mean(a_unit * g, axis=-1, keepdims=True)
    grad_attempts = (g - a_unit * inner) * a_scale
    return (loss.reshape(-1), grad_attempts, grad_weight)


def solution(mesh):
    fine = Mesh(mesh.devices.reshape(SIZES), AXES)
    slices, everyone = P(("z", "yl")), P(AXES)
    return jax.shard_map(
        on_device,
        mesh=fine,
        in_specs=(everyone, P(), everyone, slices, everyone),
        out_specs=(everyone, everyone, P()),
        check_vma=False,
    )
```

```python
import functools
import itertools

import jax
import jax.numpy as jnp
from jax import lax
from jax.experimental import pallas as pl
from jax.experimental.pallas import tpu as pltpu
from jax.sharding import Mesh, PartitionSpec as P


SHARP = 0.07
EPS = 1e-06
LOG2E = 1.4426950408889634
AXES = ("z", "yl", "yh", "x", "c")
SIZES = (8, 2, 2, 4, 2)
PLANE = ("yh", "yl", "x")
ROW = ("yh", "x")
SUB = 256
BF, F32 = jnp.bfloat16, jnp.float32
Q_TILE = 512


def flat(coords):
    index = 0
    for value, size in zip(coords, SIZES):
        index = index * size + value % size
    return index


def send(value, move):
    pairs = [(flat(at), flat(move(*at))) for at in itertools.product(*map(range, SIZES))]
    return lax.ppermute(value, AXES, pairs)


def to_core(value):
    return send(value, lambda z, yl, yh, x, c: (z, yl, yh, x, c ^ 1))


def to_z(value, where):
    return send(value, lambda z, yl, yh, x, c: (where(z), yl, yh, x, c))


def unit_kernel(attempts, spread, scale):
    a = attempts[...].astype(F32)
    r = lax.rsqrt(jnp.sum(a * a, axis=1, keepdims=True) * (1.0 / a.shape[1]) + EPS)
    u = (a * r).astype(BF)
    for k in range(spread.shape[0]):
        spread[k] = u
    scale[...] = r


def unit_rows(attempts):
    rows, width = attempts.shape
    return pl.pallas_call(
        unit_kernel,
        out_shape=[
            jax.ShapeDtypeStruct((8, rows, width), BF),
            jax.ShapeDtypeStruct((rows, 1), F32),
        ],
        cost_estimate=pl.CostEstimate(
            flops=4 * rows * width, bytes_accessed=18 * rows * width, transcendentals=0
        ),
        name="unit",
    )(attempts)


def row_ids(core, half, rows):
    r = lax.broadcasted_iota(jnp.int32, (half, 1), 0)
    return r + (r // rows + core) * rows


def proj_kernel(rows, core, states, weight, labels, positive,
                proj, query, scale, label_q, states_t, weight_t):
    @pl.when(pl.program_id(0) == 0)
    def _():
        weight_t[...] = weight[...].T

    half = labels.shape[0] // 2
    pos = positive[...]
    first = jnp.where(row_ids(core[0], half, rows) == pos, labels[:half, :], 0.0)
    second = jnp.where(row_ids(1 - core[0], half, rows) == pos, labels[half:, :], 0.0)
    label_q[...] = jnp.sum(first + second, axis=0, keepdims=True)
    states_t[...] = states[...].T
    p = jnp.dot(weight_t[...], states_t[...], preferred_element_type=F32)
    r = lax.rsqrt(jnp.sum(p * p, axis=0, keepdims=True) * (1.0 / p.shape[0]) + EPS)
    proj[...] = p
    query[...] = (p * r).astype(BF)
    scale[...] = r


def column(rows):
    return pl.BlockSpec((rows, Q_TILE), lambda i: (0, i))


def whole(shape):
    return pl.BlockSpec(shape, lambda i: (0, 0))


SCALAR = pl.BlockSpec(memory_space=pltpu.SMEM)


def project(core, states, weight, labels, positive, rows):
    queries, width = states.shape
    return pl.pallas_call(
        functools.partial(proj_kernel, rows),
        grid=(queries // Q_TILE,),
        in_specs=[
            SCALAR,
            pl.BlockSpec((Q_TILE, width), lambda i: (i, 0)),
            whole((width, width)), whole(labels.shape), column(1),
        ],
        out_specs=[column(width), column(width), column(1), column(1), column(width)],
        out_shape=[
            jax.ShapeDtypeStruct((width, queries), F32),
            jax.ShapeDtypeStruct((width, queries), BF),
            jax.ShapeDtypeStruct((1, queries), F32),
            jax.ShapeDtypeStruct((1, queries), F32),
            jax.ShapeDtypeStruct((width, queries), BF),
        ],
        scratch_shapes=[pltpu.VMEM((width, width), BF)],
        cost_estimate=pl.CostEstimate(
            flops=2 * queries * width * width,
            bytes_accessed=queries * width * 10,
            transcendentals=0,
        ),
        name="project",
    )(core, states, weight, labels, positive)


def loss_kernel(mult, rows, core, proj, query, scale, label_q, states_t, own, other,
                labels, positive, loss, weights, keep, give, own_t, other_t, total_w):
    step = pl.program_id(0)

    @pl.when(step == 0)
    def _():
        own_t[...] = own[...].T
        other_t[...] = other[...].T
        total_w[...] = jnp.zeros_like(total_w)

    half = own.shape[0]
    width = own.shape[1]
    label_a, label_b = labels[:half, :], labels[half:, :]
    ids_a = row_ids(core[0], half, rows)
    ids_b = row_ids(1 - core[0], half, rows)
    parts = []
    for k in range(Q_TILE // SUB):
        cols = slice(k * SUB, (k + 1) * SUB)
        q = query[:, cols]
        s_a = jnp.dot(own[...], q, preferred_element_type=F32)
        s_b = jnp.dot(other[...], q, preferred_element_type=F32)
        parts.append((cols, s_a, s_b))
    for cols, s_a, s_b in parts:
        pos = positive[:, cols]
        wanted = label_q[:, cols]
        chosen_a = ids_a == pos
        chosen_b = ids_b == pos
        pick = jnp.sum(jnp.where(chosen_a, s_a, 0.0), axis=0, keepdims=True)
        pick += jnp.sum(jnp.where(chosen_b, s_b, 0.0), axis=0, keepdims=True)
        e_a = jnp.where(label_a == wanted, jnp.exp2(s_a * (mult * LOG2E)), 0.0)
        e_b = jnp.where(label_b == wanted, jnp.exp2(s_b * (mult * LOG2E)), 0.0)
        total = jnp.sum(e_a, axis=0, keepdims=True) + jnp.sum(e_b, axis=0, keepdims=True)
        loss[:, cols] = jnp.log(total) - pick * mult
        inv = 1.0 / total
        w_a = (e_a * inv - jnp.where(chosen_a, 1.0, 0.0)).astype(BF)
        w_b = (e_b * inv - jnp.where(chosen_b, 1.0, 0.0)).astype(BF)
        weights[:half, cols] = w_a
        weights[half:, cols] = w_b
        g = jnp.dot(own_t[...], w_a, preferred_element_type=F32)
        g += jnp.dot(other_t[...], w_b, preferred_element_type=F32)
        r = scale[:, cols]
        u = proj[:, cols] * r
        inner = jnp.sum(u * g, axis=0, keepdims=True) * (1.0 / width)
        grad_proj = ((g - u * inner) * (r * mult)).astype(BF)
        total_w[...] += lax.dot_general(
            states_t[:, cols], grad_proj, (((1,), (1,)), ((), ())), preferred_element_type=F32
        )

    @pl.when(step == pl.num_programs(0) - 1)
    def _():
        half_w = width // 2
        keep[...] = total_w[pl.ds(pl.multiple_of(core[0] * half_w, half_w), half_w), :]
        rest = total_w[pl.ds(pl.multiple_of((1 - core[0]) * half_w, half_w), half_w), :]
        give[...] = rest.astype(BF)


def losses_and_weights(mult, core, proj, query, scale, label_q, states_t, own, other,
                       labels, positive, rows):
    width, queries = proj.shape
    half = own.shape[0]
    half_w = width // 2
    return pl.pallas_call(
        functools.partial(loss_kernel, mult, rows),
        grid=(queries // Q_TILE,),
        in_specs=[
            SCALAR, column(width), column(width), column(1), column(1), column(width),
            whole(own.shape), whole(other.shape), whole(labels.shape), column(1),
        ],
        out_specs=[column(1), column(2 * half), whole((half_w, width)), whole((half_w, width))],
        out_shape=[
            jax.ShapeDtypeStruct((1, queries), F32),
            jax.ShapeDtypeStruct((2 * half, queries), BF),
            jax.ShapeDtypeStruct((half_w, width), F32),
            jax.ShapeDtypeStruct((half_w, width), BF),
        ],
        scratch_shapes=[
            pltpu.VMEM((width, half), BF),
            pltpu.VMEM((width, half), BF),
            pltpu.VMEM((width, width), F32),
        ],
        cost_estimate=pl.CostEstimate(
            flops=8 * queries * width * half + 2 * queries * width * width,
            bytes_accessed=queries * width * 12,
            transcendentals=2 * half * queries,
        ),
        name="losses",
    )(core, proj, query, scale, label_q, states_t, own, other, labels, positive)


def on_device(states, query_weight, attempts, attempt_theorem, positive):
    width = states.shape[1]
    mult = 1.0 / (SHARP * width)
    rows = attempts.shape[0]
    c = lax.axis_index("c")
    core = c.reshape(1)

    spread_a, a_scale = unit_rows(attempts)
    own = lax.all_to_all(spread_a, ROW, 0, 0).reshape(-1, width)
    other = to_core(own)

    by_core = attempt_theorem.astype(F32).reshape(8, 2, rows)
    even, odd = by_core[:, 0].reshape(-1), by_core[:, 1].reshape(-1)
    labels = jnp.concatenate([jnp.where(c == 0, even, odd), jnp.where(c == 0, odd, even)])
    labels = labels.reshape(-1, 1)
    pos = positive.reshape(1, -1)

    proj, query, scale, label_q, states_t = project(core, states, query_weight, labels, pos, rows)
    loss, weights, w_keep, w_give = losses_and_weights(
        mult, core, proj, query, scale, label_q, states_t, own, other, labels, pos, rows
    )

    half_a = own.shape[0]
    contract = (((1,), (1,)), ((), ()))
    w_sum = (w_keep + to_core(w_give).astype(F32)).astype(BF)
    parts = lax.all_to_all(w_sum.reshape(16, -1, width), PLANE, 0, 0)
    a_give = lax.dot_general(
        weights[half_a:], query, contract, preferred_element_type=F32
    ).astype(BF)
    a_keep = lax.dot_general(weights[:half_a], query, contract, preferred_element_type=F32)
    a_sum = (a_keep + to_core(a_give).astype(F32)).astype(BF)

    piece = jnp.sum(parts.astype(F32), axis=0).astype(BF)
    a_parts = lax.all_to_all(a_sum.reshape(8, rows, width), ROW, 0, 0)
    moved = to_z(piece, lambda z: z ^ 1)
    piece = (piece.astype(F32) + moved.astype(F32)).astype(BF)
    far, up, down = (to_z(piece, lambda z, s=s: z + s) for s in (4, 2, 6))
    even = piece.astype(F32) + far.astype(F32)
    odd = up.astype(F32) + down.astype(F32)
    piece = (even + odd).astype(BF)
    a_unit = attempts.astype(F32) * a_scale
    g = jnp.sum(a_parts.astype(F32), axis=0)
    inner = jnp.mean(a_unit * g, axis=-1, keepdims=True)
    grad_attempts = (g - a_unit * inner) * (a_scale * mult)

    spread = jnp.broadcast_to(piece[None], (16,) + piece.shape)
    w_half = lax.all_to_all(spread, PLANE, 0, 0).reshape(-1, width)
    w_rest = to_core(w_half)
    low = jnp.where(c == 0, w_half, w_rest)
    high = jnp.where(c == 0, w_rest, w_half)
    grad_weight = jnp.concatenate([low, high], axis=0).astype(F32)
    return (loss.reshape(-1), grad_attempts, grad_weight)


def solution(mesh):
    fine = Mesh(mesh.devices.reshape(SIZES), AXES)
    slices, everyone = P(("z", "yl")), P(AXES)

    return jax.shard_map(
        on_device,
        mesh=fine,
        in_specs=(everyone, P(), everyone, slices, everyone),
        out_specs=(everyone, everyone, P()),
        check_vma=False,
    )
```

```python
import functools
import itertools

import jax
import jax.numpy as jnp
from jax import lax
from jax.experimental import pallas as pl
from jax.experimental.pallas import tpu as pltpu
from jax.sharding import Mesh, PartitionSpec as P


SHARP = 0.07
EPS = 1e-06
LOG2E = 1.4426950408889634
AXES = ("z", "yl", "yh", "x", "c")
SIZES = (8, 2, 2, 4, 2)
PLANE = ("yh", "yl", "x")
ROW = ("yh", "x")
BF, F32 = jnp.bfloat16, jnp.float32
Q_TILE = 512
TILE = 1024


def flat(coords):
    index = 0
    for value, size in zip(coords, SIZES):
        index = index * size + value % size
    return index


def send(value, move):
    pairs = [(flat(at), flat(move(*at))) for at in itertools.product(*map(range, SIZES))]
    return lax.ppermute(value, AXES, pairs)


def to_core(value):
    return send(value, lambda z, yl, yh, x, c: (z, yl, yh, x, c ^ 1))


def to_z(value, where):
    return send(value, lambda z, yl, yh, x, c: (where(z), yl, yh, x, c))


def unit_kernel(attempts, spread, scale):
    a = attempts[...].astype(F32)
    r = lax.rsqrt(jnp.sum(a * a, axis=1, keepdims=True) * (1.0 / a.shape[1]) + EPS)
    u = (a * r).astype(BF)
    for k in range(spread.shape[0]):
        spread[k] = u
    scale[...] = r


def unit_rows(attempts):
    rows, width = attempts.shape
    return pl.pallas_call(
        unit_kernel,
        out_shape=[
            jax.ShapeDtypeStruct((8, rows, width), BF),
            jax.ShapeDtypeStruct((rows, 1), F32),
        ],
        cost_estimate=pl.CostEstimate(
            flops=4 * rows * width, bytes_accessed=18 * rows * width, transcendentals=0
        ),
        name="unit",
    )(attempts)


def row_ids(core, half, rows):
    r = lax.broadcasted_iota(jnp.int32, (half, 1), 0)
    return r + (r // rows + core) * rows


def proj_kernel(rows, core, states, weight, labels, positive,
                query, scale, label_q, states_t, weight_t):
    @pl.when(pl.program_id(0) == 0)
    def _():
        weight_t[...] = weight[...].T

    half = labels.shape[0] // 2
    pos = positive[...]
    first = jnp.where(row_ids(core[0], half, rows) == pos, labels[:half, :], 0.0)
    second = jnp.where(row_ids(1 - core[0], half, rows) == pos, labels[half:, :], 0.0)
    label_q[...] = jnp.sum(first + second, axis=0, keepdims=True)
    states_t[...] = states[...].T
    p = jnp.dot(weight_t[...], states_t[...], preferred_element_type=F32)
    r = lax.rsqrt(jnp.sum(p * p, axis=0, keepdims=True) * (1.0 / p.shape[0]) + EPS)
    query[...] = (p * r).astype(BF)
    scale[...] = r


def column(rows):
    return pl.BlockSpec((rows, Q_TILE), lambda i: (0, i))


def whole(shape):
    return pl.BlockSpec(shape, lambda i: (0, 0))


SCALAR = pl.BlockSpec(memory_space=pltpu.SMEM)


def project(core, states, weight, labels, positive, rows):
    queries, width = states.shape
    return pl.pallas_call(
        functools.partial(proj_kernel, rows),
        grid=(queries // Q_TILE,),
        in_specs=[
            SCALAR,
            pl.BlockSpec((Q_TILE, width), lambda i: (i, 0)),
            whole((width, width)), whole(labels.shape), column(1),
        ],
        out_specs=[column(width), column(1), column(1), column(width)],
        out_shape=[
            jax.ShapeDtypeStruct((width, queries), BF),
            jax.ShapeDtypeStruct((1, queries), F32),
            jax.ShapeDtypeStruct((1, queries), F32),
            jax.ShapeDtypeStruct((width, queries), BF),
        ],
        scratch_shapes=[pltpu.VMEM((width, width), BF)],
        cost_estimate=pl.CostEstimate(
            flops=2 * queries * width * width,
            bytes_accessed=queries * width * 6,
            transcendentals=0,
        ),
        name="project",
    )(core, states, weight, labels, positive)


def loss_kernel(mult, rows, tile, core, query_hbm, states_hbm, own_hbm, other_hbm, scale, label_q, labels,
                 positive, loss, weights_hbm, keep, give,
                 panel, panel_t, query, states, weights, grad_p, acc_keep, acc_give, sems):
    half, width = own_hbm.shape
    queries = query_hbm.shape[1]
    count = queries // tile
    cols = [slice(k * tile, (k + 1) * tile) for k in range(count)]
    panel_in = [
        pltpu.make_async_copy(own_hbm, panel.at[:half, :], sems.at[0]),
        pltpu.make_async_copy(other_hbm, panel.at[half:, :], sems.at[1]),
    ]
    query_in = [
        pltpu.make_async_copy(query_hbm.at[:, c], query.at[:, c], sems.at[2 + k])
        for k, c in enumerate(cols)
    ]
    states_in = pltpu.make_async_copy(states_hbm, states, sems.at[2 + count])
    weights_out = [
        pltpu.make_async_copy(weights.at[:, c], weights_hbm.at[:, c], sems.at[3 + count + k])
        for k, c in enumerate(cols)
    ]
    for copy in panel_in + query_in + [states_in]:
        copy.start()
    ids = jnp.concatenate([row_ids(core[0], half, rows), row_ids(1 - core[0], half, rows)], axis=0)
    label_j = labels[...]
    half_w = width // 2
    mine = pl.ds(pl.multiple_of(core[0] * half_w, half_w), half_w)
    theirs = pl.ds(pl.multiple_of((1 - core[0]) * half_w, half_w), half_w)

    def scores(k):
        return jnp.dot(panel[...], query[:, cols[k]], preferred_element_type=F32)

    def soften(k, s):
        c = cols[k]
        chosen = ids == positive[:, c]
        pick = jnp.sum(jnp.where(chosen, s, 0.0), axis=0, keepdims=True)
        e = jnp.where(label_j == label_q[:, c], jnp.exp2(s * (mult * LOG2E)), 0.0)
        total = jnp.sum(e, axis=0, keepdims=True)
        loss[:, c] = jnp.log(total) - pick * mult
        w = e * (1.0 / total)
        weights[:, c] = jnp.where(chosen, w - 1.0, w).astype(BF)

    def back(k):
        c = cols[k]
        g = jnp.dot(panel_t[...], weights[:, c], preferred_element_type=F32)
        u = query[:, c].astype(F32)
        inner = jnp.sum(u * g, axis=0, keepdims=True) * (1.0 / width)
        grad_p[:, c] = ((g - u * inner) * (scale[:, c] * mult)).astype(BF)

    def weight_part(which, c):
        return lax.dot_general(
            states[which, c], grad_p[:, c], (((1,), (1,)), ((), ())), preferred_element_type=F32
        )

    for copy in panel_in:
        copy.wait()
    query_in[0].wait()
    s = scores(0)
    panel_t[:, :half] = panel[:half, :].T
    panel_t[:, half:] = panel[half:, :].T
    for k in range(count):
        later = None
        if k + 1 < count:
            query_in[k + 1].wait()
            later = scores(k + 1)
        if k >= 1:
            back(k - 1)
        soften(k, s)
        s = later
    for copy in weights_out:
        copy.start()
    states_in.wait()
    early = slice(0, (count - 1) * tile)
    acc_give[...] = weight_part(theirs, early)
    acc_keep[...] = weight_part(mine, early)
    back(count - 1)
    last = cols[count - 1]
    give[...] = (acc_give[...] + weight_part(theirs, last)).astype(BF)
    keep[...] = (acc_keep[...] + weight_part(mine, last)).astype(BF)
    for copy in weights_out:
        copy.wait()


def losses_and_weights(mult, rows, core, query, scale, label_q, states_t, own, other, labels, positive):
    width, queries = query.shape
    half = own.shape[0]
    half_w = width // 2
    count = queries // TILE
    hbm = pl.BlockSpec(memory_space=pl.ANY)
    vmem = pl.BlockSpec(memory_space=pltpu.VMEM)
    return pl.pallas_call(
        functools.partial(loss_kernel, mult, rows, TILE),
        in_specs=[pl.BlockSpec(memory_space=pltpu.SMEM), hbm, hbm, hbm, hbm, vmem, vmem, vmem, vmem],
        out_specs=[vmem, hbm, vmem, vmem],
        out_shape=[
            jax.ShapeDtypeStruct((1, queries), F32),
            jax.ShapeDtypeStruct((2 * half, queries), BF),
            jax.ShapeDtypeStruct((half_w, width), BF),
            jax.ShapeDtypeStruct((half_w, width), BF),
        ],
        scratch_shapes=[
            pltpu.VMEM((2 * half, width), BF),
            pltpu.VMEM((width, 2 * half), BF),
            pltpu.VMEM((width, queries), BF),
            pltpu.VMEM((width, queries), BF),
            pltpu.VMEM((2 * half, queries), BF),
            pltpu.VMEM((width, queries), BF),
            pltpu.VMEM((half_w, width), F32),
            pltpu.VMEM((half_w, width), F32),
            pltpu.SemaphoreType.DMA((3 + 2 * count,)),
        ],
        cost_estimate=pl.CostEstimate(
            flops=8 * queries * width * half + 2 * queries * width * width,
            bytes_accessed=queries * width * 8,
            transcendentals=2 * half * queries,
        ),
        name="losses",
    )(core, query, states_t, own, other, scale, label_q, labels, positive)


def on_device(states, query_weight, attempts, attempt_theorem, positive):
    width = states.shape[1]
    mult = 1.0 / (SHARP * width)
    rows = attempts.shape[0]
    c = lax.axis_index("c")
    core = c.reshape(1)

    spread_a, a_scale = unit_rows(attempts)
    own = lax.all_to_all(spread_a, ROW, 0, 0).reshape(-1, width)
    other = to_core(own)

    by_core = attempt_theorem.astype(F32).reshape(8, 2, rows)
    even, odd = by_core[:, 0].reshape(-1), by_core[:, 1].reshape(-1)
    labels = jnp.concatenate([jnp.where(c == 0, even, odd), jnp.where(c == 0, odd, even)])
    labels = labels.reshape(-1, 1)
    pos = positive.reshape(1, -1)

    query, scale, label_q, states_t = project(
        core, states, query_weight, labels, pos, rows
    )
    loss, weights, w_keep, w_give = losses_and_weights(
        mult, rows, core, query, scale, label_q, states_t, own, other, labels, pos
    )

    half_a = own.shape[0]
    contract = (((1,), (1,)), ((), ()))
    w_sum = (w_keep.astype(F32) + to_core(w_give).astype(F32)).astype(BF)
    parts = lax.all_to_all(w_sum.reshape(16, -1, width), PLANE, 0, 0)
    a_give = lax.dot_general(
        weights[half_a:], query, contract, preferred_element_type=F32
    ).astype(BF)
    a_keep = lax.dot_general(weights[:half_a], query, contract, preferred_element_type=F32)
    a_sum = (a_keep + to_core(a_give).astype(F32)).astype(BF)

    piece = jnp.sum(parts.astype(F32), axis=0).astype(BF)
    a_parts = lax.all_to_all(a_sum.reshape(8, rows, width), ROW, 0, 0)
    moved = to_z(piece, lambda z: z ^ 1)
    piece = (piece.astype(F32) + moved.astype(F32)).astype(BF)
    far, up, down = (to_z(piece, lambda z, s=s: z + s) for s in (4, 2, 6))
    even = piece.astype(F32) + far.astype(F32)
    odd = up.astype(F32) + down.astype(F32)
    piece = (even + odd).astype(BF)
    a_unit = attempts.astype(F32) * a_scale
    g = jnp.sum(a_parts.astype(F32), axis=0)
    inner = jnp.mean(a_unit * g, axis=-1, keepdims=True)
    grad_attempts = (g - a_unit * inner) * (a_scale * mult)

    spread = jnp.broadcast_to(piece[None], (16,) + piece.shape)
    w_half = lax.all_to_all(spread, PLANE, 0, 0).reshape(-1, width)
    w_rest = to_core(w_half)
    low = jnp.where(c == 0, w_half, w_rest)
    high = jnp.where(c == 0, w_rest, w_half)
    grad_weight = jnp.concatenate([low, high], axis=0).astype(F32)
    return (loss.reshape(-1), grad_attempts, grad_weight)


def solution(mesh):
    fine = Mesh(mesh.devices.reshape(SIZES), AXES)
    slices, everyone = P(("z", "yl")), P(AXES)

    return jax.shard_map(
        on_device,
        mesh=fine,
        in_specs=(everyone, P(), everyone, slices, everyone),
        out_specs=(everyone, everyone, P()),
        check_vma=False,
    )
```

```python
import functools
import itertools

import jax
import jax.numpy as jnp
from jax import lax
from jax.experimental import pallas as pl
from jax.experimental.pallas import tpu as pltpu
from jax.sharding import Mesh, PartitionSpec as P


SHARP = 0.07
EPS = 1e-06
LOG2E = 1.4426950408889634
AXES = ("z", "yl", "yh", "x", "c")
SIZES = (8, 2, 2, 4, 2)
PLANE = ("yh", "yl", "x")
ROW = ("yh", "x")
BF, F32 = jnp.bfloat16, jnp.float32
Q_TILE = 512
TILE = 1024


def flat(coords):
    index = 0
    for value, size in zip(coords, SIZES):
        index = index * size + value % size
    return index


def send(value, move):
    pairs = [(flat(at), flat(move(*at))) for at in itertools.product(*map(range, SIZES))]
    return lax.ppermute(value, AXES, pairs)


def to_core(value):
    return send(value, lambda z, yl, yh, x, c: (z, yl, yh, x, c ^ 1))


def to_z(value, where):
    return send(value, lambda z, yl, yh, x, c: (where(z), yl, yh, x, c))


def unit_kernel(attempts, spread, scale):
    a = attempts[...].astype(F32)
    r = lax.rsqrt(jnp.sum(a * a, axis=1, keepdims=True) * (1.0 / a.shape[1]) + EPS)
    u = (a * r).astype(BF)
    for k in range(spread.shape[0]):
        spread[k] = u
    scale[...] = r


def unit_rows(attempts):
    rows, width = attempts.shape
    return pl.pallas_call(
        unit_kernel,
        out_shape=[
            jax.ShapeDtypeStruct((8, rows, width), BF),
            jax.ShapeDtypeStruct((rows, 1), F32),
        ],
        cost_estimate=pl.CostEstimate(
            flops=4 * rows * width, bytes_accessed=18 * rows * width, transcendentals=0
        ),
        name="unit",
    )(attempts)


def row_ids(core, half, rows):
    r = lax.broadcasted_iota(jnp.int32, (half, 1), 0)
    return r + (r // rows + core) * rows


def proj_kernel(rows, core, states, weight, labels, positive,
                query, scale, label_q, states_t, weight_t):
    @pl.when(pl.program_id(0) == 0)
    def _():
        weight_t[...] = weight[...].T

    half = labels.shape[0] // 2
    pos = positive[...]
    first = jnp.where(row_ids(core[0], half, rows) == pos, labels[:half, :], 0.0)
    second = jnp.where(row_ids(1 - core[0], half, rows) == pos, labels[half:, :], 0.0)
    label_q[...] = jnp.sum(first + second, axis=0, keepdims=True)
    states_t[...] = states[...].T
    p = jnp.dot(weight_t[...], states_t[...], preferred_element_type=F32)
    r = lax.rsqrt(jnp.sum(p * p, axis=0, keepdims=True) * (1.0 / p.shape[0]) + EPS)
    query[...] = (p * r).astype(BF)
    scale[...] = r


def column(rows):
    return pl.BlockSpec((rows, Q_TILE), lambda i: (0, i))


def whole(shape):
    return pl.BlockSpec(shape, lambda i: (0, 0))


SCALAR = pl.BlockSpec(memory_space=pltpu.SMEM)


def project(core, states, weight, labels, positive, rows):
    queries, width = states.shape
    return pl.pallas_call(
        functools.partial(proj_kernel, rows),
        grid=(queries // Q_TILE,),
        in_specs=[
            SCALAR,
            pl.BlockSpec((Q_TILE, width), lambda i: (i, 0)),
            whole((width, width)), whole(labels.shape), column(1),
        ],
        out_specs=[column(width), column(1), column(1), column(width)],
        out_shape=[
            jax.ShapeDtypeStruct((width, queries), BF),
            jax.ShapeDtypeStruct((1, queries), F32),
            jax.ShapeDtypeStruct((1, queries), F32),
            jax.ShapeDtypeStruct((width, queries), BF),
        ],
        scratch_shapes=[pltpu.VMEM((width, width), BF)],
        cost_estimate=pl.CostEstimate(
            flops=2 * queries * width * width,
            bytes_accessed=queries * width * 6,
            transcendentals=0,
        ),
        name="project",
    )(core, states, weight, labels, positive)


def loss_kernel(mult, rows, tile, core, query_hbm, states_hbm, own, other, scale, label_q, labels,
                 positive, loss, weights_hbm, keep, give,
                 panel, panel_t, query, states, weights, grad_p, acc_keep, acc_give, sems):
    half, width = own.shape
    queries = query_hbm.shape[1]
    count = queries // tile
    cols = [slice(k * tile, (k + 1) * tile) for k in range(count)]
    query_in = [
        pltpu.make_async_copy(query_hbm.at[:, c], query.at[:, c], sems.at[k])
        for k, c in enumerate(cols)
    ]
    states_in = pltpu.make_async_copy(states_hbm, states, sems.at[count])
    weights_out = [
        pltpu.make_async_copy(weights.at[:, c], weights_hbm.at[:, c], sems.at[1 + count + k])
        for k, c in enumerate(cols)
    ]
    for copy in query_in + [states_in]:
        copy.start()
    ids = jnp.concatenate([row_ids(core[0], half, rows), row_ids(1 - core[0], half, rows)], axis=0)
    label_j = labels[...]
    half_w = width // 2
    mine = pl.ds(pl.multiple_of(core[0] * half_w, half_w), half_w)
    theirs = pl.ds(pl.multiple_of((1 - core[0]) * half_w, half_w), half_w)

    def scores(k):
        return jnp.dot(panel[...], query[:, cols[k]], preferred_element_type=F32)

    def soften(k, s):
        c = cols[k]
        chosen = ids == positive[:, c]
        pick = jnp.sum(jnp.where(chosen, s, 0.0), axis=0, keepdims=True)
        e = jnp.where(label_j == label_q[:, c], jnp.exp2(s * (mult * LOG2E)), 0.0)
        total = jnp.sum(e, axis=0, keepdims=True)
        loss[:, c] = jnp.log(total) - pick * mult
        w = e * (1.0 / total)
        weights[:, c] = jnp.where(chosen, w - 1.0, w).astype(BF)

    def back(k):
        c = cols[k]
        g = jnp.dot(panel_t[...], weights[:, c], preferred_element_type=F32)
        u = query[:, c].astype(F32)
        inner = jnp.sum(u * g, axis=0, keepdims=True) * (1.0 / width)
        grad_p[:, c] = ((g - u * inner) * (scale[:, c] * mult)).astype(BF)

    def weight_part(which, c):
        return lax.dot_general(
            states[which, c], grad_p[:, c], (((1,), (1,)), ((), ())), preferred_element_type=F32
        )

    panel[:half, :] = own[...]
    panel[half:, :] = other[...]
    query_in[0].wait()
    s = scores(0)
    panel_t[:, :half] = own[...].T
    panel_t[:, half:] = other[...].T
    for k in range(count):
        later = None
        if k + 1 < count:
            query_in[k + 1].wait()
            later = scores(k + 1)
        if k >= 1:
            back(k - 1)
        soften(k, s)
        s = later
    for copy in weights_out:
        copy.start()
    states_in.wait()
    early = slice(0, (count - 1) * tile)
    acc_give[...] = weight_part(theirs, early)
    acc_keep[...] = weight_part(mine, early)
    back(count - 1)
    last = cols[count - 1]
    give[...] = (acc_give[...] + weight_part(theirs, last)).astype(BF)
    keep[...] = (acc_keep[...] + weight_part(mine, last)).astype(BF)
    for copy in weights_out:
        copy.wait()


def losses_and_weights(mult, rows, core, query, scale, label_q, states_t, own, other, labels, positive):
    width, queries = query.shape
    half = own.shape[0]
    half_w = width // 2
    count = queries // TILE
    hbm = pl.BlockSpec(memory_space=pl.ANY)
    vmem = pl.BlockSpec(memory_space=pltpu.VMEM)
    return pl.pallas_call(
        functools.partial(loss_kernel, mult, rows, TILE),
        in_specs=[pl.BlockSpec(memory_space=pltpu.SMEM), hbm, hbm, vmem, vmem, vmem, vmem, vmem, vmem],
        out_specs=[vmem, hbm, vmem, vmem],
        out_shape=[
            jax.ShapeDtypeStruct((1, queries), F32),
            jax.ShapeDtypeStruct((2 * half, queries), BF),
            jax.ShapeDtypeStruct((half_w, width), BF),
            jax.ShapeDtypeStruct((half_w, width), BF),
        ],
        scratch_shapes=[
            pltpu.VMEM((2 * half, width), BF),
            pltpu.VMEM((width, 2 * half), BF),
            pltpu.VMEM((width, queries), BF),
            pltpu.VMEM((width, queries), BF),
            pltpu.VMEM((2 * half, queries), BF),
            pltpu.VMEM((width, queries), BF),
            pltpu.VMEM((half_w, width), F32),
            pltpu.VMEM((half_w, width), F32),
            pltpu.SemaphoreType.DMA((1 + 2 * count,)),
        ],
        cost_estimate=pl.CostEstimate(
            flops=8 * queries * width * half + 2 * queries * width * width,
            bytes_accessed=queries * width * 8,
            transcendentals=2 * half * queries,
        ),
        compiler_params=pltpu.CompilerParams(vmem_limit_bytes=44 * 2**20),
        name="losses",
    )(core, query, states_t, own, other, scale, label_q, labels, positive)


def on_device(states, query_weight, attempts, attempt_theorem, positive):
    width = states.shape[1]
    mult = 1.0 / (SHARP * width)
    rows = attempts.shape[0]
    c = lax.axis_index("c")
    core = c.reshape(1)

    spread_a, a_scale = unit_rows(attempts)
    own = lax.all_to_all(spread_a, ROW, 0, 0).reshape(-1, width)
    other = to_core(own)

    by_core = attempt_theorem.astype(F32).reshape(8, 2, rows)
    even, odd = by_core[:, 0].reshape(-1), by_core[:, 1].reshape(-1)
    labels = jnp.concatenate([jnp.where(c == 0, even, odd), jnp.where(c == 0, odd, even)])
    labels = labels.reshape(-1, 1)
    pos = positive.reshape(1, -1)

    query, scale, label_q, states_t = project(
        core, states, query_weight, labels, pos, rows
    )
    loss, weights, w_keep, w_give = losses_and_weights(
        mult, rows, core, query, scale, label_q, states_t, own, other, labels, pos
    )

    half_a = own.shape[0]
    contract = (((1,), (1,)), ((), ()))
    w_sum = (w_keep.astype(F32) + to_core(w_give).astype(F32)).astype(BF)
    parts = lax.all_to_all(w_sum.reshape(16, -1, width), PLANE, 0, 0)
    a_give = lax.dot_general(
        weights[half_a:], query, contract, preferred_element_type=F32
    ).astype(BF)
    a_keep = lax.dot_general(weights[:half_a], query, contract, preferred_element_type=F32)
    a_sum = (a_keep + to_core(a_give).astype(F32)).astype(BF)

    piece = jnp.sum(parts.astype(F32), axis=0).astype(BF)
    a_parts = lax.all_to_all(a_sum.reshape(8, rows, width), ROW, 0, 0)
    moved = to_z(piece, lambda z: z ^ 1)
    piece = (piece.astype(F32) + moved.astype(F32)).astype(BF)
    far, up, down = (to_z(piece, lambda z, s=s: z + s) for s in (4, 2, 6))
    even = piece.astype(F32) + far.astype(F32)
    odd = up.astype(F32) + down.astype(F32)
    piece = (even + odd).astype(BF)
    a_unit = attempts.astype(F32) * a_scale
    g = jnp.sum(a_parts.astype(F32), axis=0)
    inner = jnp.mean(a_unit * g, axis=-1, keepdims=True)
    grad_attempts = (g - a_unit * inner) * (a_scale * mult)

    spread = jnp.broadcast_to(piece[None], (16,) + piece.shape)
    w_half = lax.all_to_all(spread, PLANE, 0, 0).reshape(-1, width)
    w_rest = to_core(w_half)
    low = jnp.where(c == 0, w_half, w_rest)
    high = jnp.where(c == 0, w_rest, w_half)
    grad_weight = jnp.concatenate([low, high], axis=0).astype(F32)
    return (loss.reshape(-1), grad_attempts, grad_weight)


def solution(mesh):
    fine = Mesh(mesh.devices.reshape(SIZES), AXES)
    slices, everyone = P(("z", "yl")), P(AXES)

    return jax.shard_map(
        on_device,
        mesh=fine,
        in_specs=(everyone, P(), everyone, slices, everyone),
        out_specs=(everyone, everyone, P()),
        check_vma=False,
    )
```
